32 devices in a mesh: arc: 8 (over y, x, core), coef: 4 (over z).
Axes of the slice: x: 2, y: 2, z: 4, core: 2. Of those that a mesh axis runs over, the one named last changes fastest.
Arguments:
- design: float32 [4096, 16384], P('arc', 'coef'), may hold values from -0.046875 to 0.046875
- observations: float32 [256, 4096], P('coef', 'arc'), may hold values from -30 to 30, as said below
- start_coefs: float32 [256, 16384], P('arc', 'coef'), may hold values from -3 to 3
- precond: float32 [16384], P('coef'), may hold values from 0.3 to 1.5
- taps: float32 [128], replicated, may hold values from -0.4 to 0.4
Outputs:
- coefs: float32 [256, 16384], P('arc', 'coef')
- misfit: float32 [256, 4096], P('coef', 'arc')
The draws below stay inside these ranges and needn't reach their ends.
Inputs may be any that keep to these rules, and one draw needn't show every extreme that they name: `observations`: observations of a satellite mission with a noise level that varies along time and occasional outliers.
All inputs are finite; a program needn't handle non-finite values.
Results may differ from the reference program's by a relative error of at most 0.00026.
Values sent between devices are 32-bit elements; how exact they have to be, the bound alone decides.
No kernel may reach another device: no remote copies, remote signals or barrier semaphores. Data moves between devices by JAX's collectives and lax.ppermute only.
A program may use at most 64 MiB of HBM per device.

```python
import math
import jax
import jax.numpy as jnp
from jax import lax

NCOEF = 16384
NRHS = 256
TAPS = 128
ITERS = 2
NOBS = 4096


def draw_observations(key, part):
    keys = jax.random.split(jax.random.fold_in(key, 11), 4)
    moment = jnp.arange(NOBS, dtype=jnp.float32) / NOBS
    trend = jnp.exp(moment * jnp.log(3.0))
    rough = jnp.exp(jax.random.uniform(keys[1], (NOBS,), minval=-0.7, maxval=0.7))
    base = jax.random.normal(keys[0], (NRHS, NOBS))
    spikes = (jax.random.uniform(keys[2], (NRHS, NOBS)) < 0.02).astype(jnp.float32)
    outliers = spikes * 6.0 * jax.random.normal(keys[3], (NRHS, NOBS))
    values = 0.6 * base * trend[None, :] * rough[None, :] + outliers
    return jnp.clip(values, -30.0, 30.0).astype(jnp.float32)


def block_levels(own_key, extent, cuts, smallest, largest):
    def one(dim, shards_of):
        steps = jax.random.uniform(jax.random.fold_in(jax.random.fold_in(own_key, 6), dim), (shards_of,), jnp.float32, smallest / len(cuts), largest / len(cuts))
        return jnp.repeat(jnp.exp(steps), extent[dim] // shards_of).reshape((-1,) + (1,) * (len(extent) - dim - 1))

    gain = one(*cuts[0])
    for cut in cuts[1:]:
        gain = gain * one(*cut)
    return gain


def centred(key, dims, deviation, bound, pieces=(), kind=jnp.bfloat16):
    values = deviation * jax.random.normal(key, dims, jnp.float32)
    if pieces:
        values = values * block_levels(key, dims, pieces, -0.22, 0.18)
    return jnp.clip(values, -bound, bound).astype(kind)


def setup_inputs(seed: int = 0) -> dict:
    streams_of = jax.random.split(jax.random.key(seed), 6)
    return {
        "design": centred(streams_of[0], (NOBS, NCOEF), NCOEF ** -0.5, 0.046875, ((0, 8), (1, 4)), jnp.float32),
        "observations": draw_observations(jax.random.fold_in(streams_of[5], 71), 0),
        "start_coefs": centred(streams_of[2], (NRHS, NCOEF), 0.5, 3.0, ((0, 8), (1, 4)), jnp.float32),
        "precond": jnp.clip(jnp.exp(math.log(1.5) - 1.60943787 * jax.random.uniform(streams_of[3], (NCOEF,), jnp.float32) ** block_levels(streams_of[3], (NCOEF,), ((0, 4),), -0.2, 0.2)), 0.3, 1.5),
        "taps": centred(streams_of[4], (TAPS,), 0.08, 0.4, (), jnp.float32),
    }


huber_square = 2.25
epsilon = 1e-06

def make_filters(taps):
    filt = taps.at[0].add(1.0)
    source = jnp.arange(TAPS)[:, None]
    target = jnp.arange(TAPS)[None, :]
    offset = target - source
    first = jnp.where(offset >= 0, filt[jnp.clip(offset, 0, TAPS - 1)], 0.0)
    second = jnp.where(offset < 0, filt[jnp.clip(offset + TAPS, 0, TAPS - 1)], 0.0)
    return (first, second)

def whiten(values, edge, first, second):
    blocks = values.reshape(values.shape[0], -1, TAPS)
    before = jnp.concatenate([edge[:, None, :], blocks[:, :-1]], axis=1)
    result = jnp.einsum('kjs,st->kjt', blocks, first, precision=lax.Precision.HIGHEST)
    result = result + jnp.einsum('kjs,st->kjt', before, second, precision=lax.Precision.HIGHEST)
    return result.reshape(values.shape)

def whiten_back(values, edge, first, second):
    blocks = values.reshape(values.shape[0], -1, TAPS)
    after = jnp.concatenate([blocks[:, 1:], edge[:, None, :]], axis=1)
    result = jnp.einsum('kjt,st->kjs', blocks, first, precision=lax.Precision.HIGHEST)
    result = result + jnp.einsum('kjt,st->kjs', after, second, precision=lax.Precision.HIGHEST)
    return result.reshape(values.shape)

def reference(design, observations, start_coefs, precond, taps):
    first, second = make_filters(taps)
    zero_edge = jnp.zeros((NRHS, TAPS), jnp.float32)
    coefs = start_coefs
    predicted = jnp.dot(coefs, design.T, precision=lax.Precision.HIGHEST, preferred_element_type=jnp.float32)
    direction = jnp.zeros_like(coefs)
    previous_gp = jnp.ones((NRHS,), jnp.float32)
    for iteration in range(ITERS):
        residual = observations - predicted
        whitened = whiten(residual, zero_edge, first, second)
        scale = lax.optimization_barrier(jnp.sum(whitened * whitened, axis=1)) / NOBS
        weights = 1.0 / jnp.sqrt(1.0 + whitened * whitened / (huber_square * scale[:, None] + epsilon))
        back = whiten_back(weights * whitened, zero_edge, first, second)
        gradient = jnp.dot(back, design, precision=lax.Precision.HIGHEST, preferred_element_type=jnp.float32)
        conditioned = precond[None, :] * gradient
        grad_prod = lax.optimization_barrier(jnp.sum(gradient * conditioned, axis=1))
        grad_old = lax.optimization_barrier(jnp.sum(gradient * direction, axis=1))
        if iteration == 0:
            direction = conditioned
            grad_dir = grad_prod
        else:
            beta = grad_prod / previous_gp
            direction = conditioned + beta[:, None] * direction
            grad_dir = grad_prod + beta * grad_old
        image = jnp.dot(direction, design.T, precision=lax.Precision.HIGHEST, preferred_element_type=jnp.float32)
        imaged = whiten(image, zero_edge, first, second)
        curvature = lax.optimization_barrier(jnp.sum(weights * imaged * imaged, axis=1))
        alpha = grad_dir / curvature
        coefs = coefs + alpha[:, None] * direction
        predicted = predicted + alpha[:, None] * image
        previous_gp = grad_prod
    return (coefs, observations - predicted)
```

```python
import functools

import jax
import jax.numpy as jnp
from jax import lax
from jax.sharding import Mesh
from jax.sharding import PartitionSpec as P

ITERS = 2

huber_square = 2.25
epsilon = 1e-06


def pieces(values):
    high = lax.reduce_precision(values, 8, 7)
    return high.astype(jnp.bfloat16), (values - high).astype(jnp.bfloat16)


def product(left, right, dims):
    def one(a, b):
        return lax.dot_general(a, b, (dims, ((), ())), preferred_element_type=jnp.float32)

    return one(left[0], right[0]) + (one(left[0], right[1]) + one(left[1], right[0]))


def make_filters(taps):
    length = taps.shape[0]
    filt = taps.at[0].add(1.0)
    zero = jnp.zeros_like(filt)

    def toeplitz(line):
        flat = jnp.tile(line, length)[: length * (2 * length - 1)]
        return flat.reshape(length, 2 * length - 1)[:, :length]

    return toeplitz(jnp.concatenate([filt, zero])), toeplitz(jnp.concatenate([zero, filt]))


def conv(blocks, matrix, transposed):
    spec = "kjt,st->kjs" if transposed else "kjs,st->kjt"
    return jnp.einsum(spec, blocks, matrix, precision=lax.Precision.HIGHEST)


def whiten(values, first, second):
    length = first.shape[0]
    blocks = values.reshape(values.shape[0], -1, length)
    before = jnp.pad(blocks[:, :-1], ((0, 0), (1, 0), (0, 0)))
    return (conv(blocks, first, False) + conv(before, second, False)).reshape(values.shape)


def whiten_back(values, first, second):
    length = first.shape[0]
    blocks = values.reshape(values.shape[0], -1, length)
    after = jnp.pad(blocks[:, 1:], ((0, 0), (0, 1), (0, 0)))
    return (conv(blocks, first, True) + conv(after, second, True)).reshape(values.shape)


def flip(values, axis, mask):
    count = lax.axis_size(axis)
    return lax.ppermute(values, axis, [(i, i ^ mask) for i in range(count)])


def rows_of(values, index, size):
    return lax.dynamic_slice_in_dim(values, index * size, size, 0)


def place(parts, me, axis):
    size = parts[0].shape[axis]
    shape = list(parts[0].shape)
    shape[axis] = size * len(parts)
    whole = jnp.zeros(shape, parts[0].dtype)
    for j, part in enumerate(parts):
        whole = lax.dynamic_update_slice_in_dim(whole, part, (me ^ j) * size, axis)
    return whole


def gather_chips(part_list):
    bits = (lax.axis_size("chip") - 1).bit_length()
    held = [{0: part} for part in part_list]
    for step in range(bits):
        for number, blocks in enumerate(held):
            mask = 1 << ((number + step) % bits)
            for j in sorted(blocks):
                blocks[j ^ mask] = flip(blocks[j], "chip", mask)
    return held


def scatter_chips(part_list):
    bits = (lax.axis_size("chip") - 1).bit_length()
    for step in reversed(range(bits)):
        for number, blocks in enumerate(part_list):
            mask = 1 << ((number + step) % bits)
            for j in sorted(blocks, reverse=True):
                if j & mask:
                    blocks[j ^ mask] = blocks[j ^ mask] + flip(blocks.pop(j), "chip", mask)
    return [blocks[0] for blocks in part_list]


def body(design, observations, start_coefs, precond, taps):
    chips = lax.axis_size("chip")
    layers = lax.axis_size("coef")
    chip = lax.axis_index("chip")
    core = lax.axis_index("core")
    layer = lax.axis_index("coef")
    half = design.shape[1] // 2
    step = design.shape[0]
    span = 2 * step
    total_obs = span * chips
    first, second = make_filters(taps)

    def both(values, axis):
        size = values.shape[axis] // 2
        keep = lax.dynamic_slice_in_dim(values, core * size, size, axis)
        send = lax.dynamic_slice_in_dim(values, (1 - core) * size, size, axis)
        return keep, flip(send, "core", 1)

    def swap(values, split, join):
        keep, other = both(values, split)
        low = jnp.where(core == 0, keep, other)
        high = jnp.where(core == 0, other, keep)
        return jnp.concatenate([low, high], axis=join)

    def forward(own):
        cut = half // 2
        held = gather_chips([own[:, :cut], own[:, cut:]])
        gathered = jnp.concatenate(
            [
                jnp.concatenate([blocks[j] for blocks in held], axis=1)
                for j in range(chips)
            ],
            axis=0,
        )
        partial = product(pieces(gathered), tiles, ((1,), (1,)))
        partial = place(
            [partial[j * own.shape[0] : (j + 1) * own.shape[0]] for j in range(chips)], chip, 0
        )
        group = partial.shape[0] // (2 * layers)
        partial = partial.reshape(layers, 2, group, span)
        keep, other = both(partial, 1)
        partial = (keep + other).reshape(layers * group, span)
        summed = rows_of(partial, layer, group)
        for j in range(1, layers):
            summed = summed + flip(rows_of(partial, layer ^ j, group), "coef", j)
        return to_time(summed)

    def to_time(block):
        few = block.shape[0] // chips
        parts = [rows_of(block, chip, few)]
        for j in range(1, chips):
            parts.append(flip(rows_of(block, chip ^ j, few), "chip", j))
        return place(parts, chip, 1)

    def from_time(values):
        parts = [lax.dynamic_slice_in_dim(values, chip * span, span, 1)]
        for j in range(1, chips):
            parts.append(
                flip(lax.dynamic_slice_in_dim(values, (chip ^ j) * span, span, 1), "chip", j)
            )
        return place(parts, chip, 0)

    def backward(back):
        block = from_time(back)
        parts = [block] + [flip(block, "coef", j) for j in range(1, layers)]
        block = place(parts, layer, 0)
        other = flip(block, "core", 1)
        low = jnp.where(core == 0, block, other).reshape(layers, 1, -1, span)
        high = jnp.where(core == 0, other, block).reshape(layers, 1, -1, span)
        block = jnp.concatenate([low, high], axis=1).reshape(-1, span)
        rows = block.shape[0] // chips
        block = jnp.concatenate([rows_of(block, chip ^ j, rows) for j in range(chips)], axis=0)
        block = pieces(block)
        cut = half // 2
        lists = []
        for number in range(2):
            piece = tuple(tile[:, number * cut : (number + 1) * cut] for tile in tiles)
            partial = product(block, piece, ((1,), (0,)))
            lists.append({j: partial[j * rows : (j + 1) * rows] for j in range(chips)})
        return jnp.concatenate(scatter_chips(lists), axis=1)

    own_start = swap(start_coefs, 1, 0)
    keep, other = both(design, 1)
    low = jnp.where(core == 0, keep, other)
    high = jnp.where(core == 0, other, keep)
    tiles = lax.optimization_barrier(pieces(jnp.concatenate([low, high], axis=0)))
    scale_own = lax.dynamic_slice_in_dim(precond, core * half, half, 0)

    target = to_time(swap(observations, 0, 1))
    predicted = forward(own_start)
    kept = []
    for iteration in range(ITERS):
        residual = target - predicted
        whitened = whiten(residual, first, second)
        scale = jnp.sum(whitened * whitened, axis=1) / total_obs
        weights = 1.0 / jnp.sqrt(
            1.0 + whitened * whitened / (huber_square * scale[:, None] + epsilon)
        )
        back = whiten_back(weights * whitened, first, second)
        gradient = backward(back)
        conditioned = scale_own[None, :] * gradient
        kept.append(swap(conditioned, 0, 1))
        image = forward(conditioned)
        grad_prod = jnp.sum(back * image, axis=1)
        if iteration == 0:
            grad_dir = grad_prod
            mix = [jnp.ones_like(grad_prod)]
        else:
            beta = grad_prod / previous_gp
            grad_dir = grad_prod + beta * jnp.sum(back * previous_image, axis=1)
            image = image + beta[:, None] * previous_image
            mix = [beta * m for m in mix] + [jnp.ones_like(beta)]
        imaged = whiten(image, first, second)
        curvature = jnp.sum(weights * imaged * imaged, axis=1)
        alpha = grad_dir / curvature
        predicted = predicted + alpha[:, None] * image
        previous_gp = grad_prod
        previous_image = image
        shares = [alpha * m for m in mix]
        if iteration == 0:
            total = shares
        else:
            total = [t + s for t, s in zip(total, shares)] + shares[len(total) :]
    misfit = target - predicted

    ratio = layers // chips
    lanes = jnp.stack(total, axis=1)
    lanes = jnp.pad(lanes, ((0, 0), (0, 128 - lanes.shape[1])))
    table = [None] * layers
    for s in range(layers):
        pairs = []
        for c in range(chips):
            for z in range(layers):
                spot = (c + chips * (z % ratio)) ^ s
                pairs.append((c * layers + z, (z // ratio) * layers + spot))
        table[s] = lax.ppermute(lanes, ("chip", "coef"), pairs)
    stacked = place(table, layer, 0).reshape(ratio, chips, -1, 128)
    other = flip(stacked, "core", 1)
    low = jnp.where(core == 0, stacked, other)
    high = jnp.where(core == 0, other, stacked)
    steps = jnp.stack([low, high], axis=1).reshape(-1, 128)
    steps = rows_of(steps, core, start_coefs.shape[0])
    coefs = start_coefs
    for number, part in enumerate(kept):
        coefs = coefs + steps[:, number : number + 1] * part
    misfit = swap(from_time(misfit), 1, 0)
    return coefs, misfit


def solution(mesh):
    arcs, layers = mesh.devices.shape
    inner = Mesh(mesh.devices.reshape(arcs // 2, 2, layers), ("chip", "core", "coef"))
    arc = ("chip", "core")
    placed = (P(arc, "coef"), P("coef", arc), P(arc, "coef"), P("coef"), P())
    return jax.shard_map(
        body,
        mesh=inner,
        in_specs=placed,
        out_specs=(P(arc, "coef"), P("coef", arc)),
        check_vma=False,
    )
```

```python
import jax
import jax.numpy as jnp
from jax import lax
from jax.experimental import pallas as pl
from jax.experimental.pallas import tpu as pltpu
from jax.sharding import Mesh
from jax.sharding import PartitionSpec as P

PALLAS = True

huber_square = 2.25
epsilon = 1e-06


def pieces(values):
    high = lax.reduce_precision(values, 8, 7)
    return high.astype(jnp.bfloat16), (values - high).astype(jnp.bfloat16)


def product(left, right, dims):
    def one(a, b):
        return lax.dot_general(a, b, (dims, ((), ())), preferred_element_type=jnp.float32)

    rows = left[0].shape[0]
    tall = one(jnp.concatenate(left, axis=0), right[0])
    return tall[:rows] + (tall[rows:] + one(left[0], right[1]))


def make_filters(taps):
    length = taps.shape[0]
    filt = taps.at[0].add(1.0)
    zero = jnp.zeros_like(filt)

    def toeplitz(line):
        flat = jnp.tile(line, length)[: length * (2 * length - 1)]
        return flat.reshape(length, 2 * length - 1)[:, :length]

    first = toeplitz(jnp.concatenate([filt, zero]))
    second = toeplitz(jnp.concatenate([zero, filt]))
    ahead = jnp.concatenate([second, first], axis=0)
    behind = jnp.concatenate([first.T, second.T], axis=0)
    return ahead, behind


def conv(values, matrix):
    rows, length = values.shape[0], matrix.shape[1]
    blocks = values.shape[1] // length - 1
    stacked = jnp.concatenate(
        [values[:, b * length : (b + 2) * length] for b in range(blocks)], axis=0
    )
    result = jnp.dot(
        stacked, matrix, precision=lax.Precision.HIGHEST, preferred_element_type=jnp.float32
    )
    return jnp.concatenate([result[b * rows : (b + 1) * rows] for b in range(blocks)], axis=1)


def to_table(columns, length):
    wide = jnp.concatenate(columns, axis=1)
    wide = jnp.pad(wide, ((0, 0), (0, length - wide.shape[1])))
    return wide.T[:8]


def from_table(parts):
    total = parts[0]
    for part in parts[1:]:
        total = total + part
    return total.T


def spread_kernel(fn, layers, shapes, spots, shared, *groups):
    count = len(shared)

    def kernel(spots_ref, *refs):
        values = [ref[...] for ref in refs[:count]]
        blocks, outs = refs[count : count + layers * len(groups)], refs[count + layers * len(groups) :]
        whole, high, low = outs[:3]
        for s in range(layers):
            back, kept = fn(values, [blocks[g * layers + s][...] for g in range(len(groups))])
            rows = back.shape[0]
            at = pl.ds(pl.multiple_of(spots_ref[s], rows), rows)
            whole[at, :] = back
            top = back.astype(jnp.bfloat16)
            high[at, :] = top
            low[at, :] = (back - top.astype(jnp.float32)).astype(jnp.bfloat16)
            if s == 0:
                for ref, value in zip(outs[3:], kept):
                    ref[...] = value

    rows, step = shapes[0]
    full = (rows * layers, step)
    out_shape = [
        jax.ShapeDtypeStruct(full, jnp.float32),
        jax.ShapeDtypeStruct(full, jnp.bfloat16),
        jax.ShapeDtypeStruct(full, jnp.bfloat16),
    ] + [jax.ShapeDtypeStruct(shape, jnp.float32) for shape in shapes]
    whole = pl.BlockSpec(memory_space=pltpu.VMEM)
    args = list(shared) + [block for group in groups for block in group]
    return pl.pallas_call(
        kernel,
        out_shape=tuple(out_shape),
        in_specs=[pl.BlockSpec(memory_space=pltpu.SMEM)] + [whole] * len(args),
        out_specs=(whole,) * len(out_shape),
        compiler_params=pltpu.CompilerParams(vmem_limit_bytes=24 * 1024 * 1024),
    )(spots, *args)


def dot_rows(a, b):
    return jnp.sum(a * b, axis=1, keepdims=True)


def local(fn, shapes, *args):
    if not PALLAS:
        return fn(*args)

    def kernel(*refs):
        outs = fn(*[ref[...] for ref in refs[: len(args)]])
        for ref, value in zip(refs[len(args) :], outs):
            ref[...] = value

    whole = pl.BlockSpec(memory_space=pltpu.VMEM)
    return pl.pallas_call(
        kernel,
        out_shape=tuple(jax.ShapeDtypeStruct(s, jnp.float32) for s in shapes),
        in_specs=[whole] * len(args),
        out_specs=(whole,) * len(shapes),
        compiler_params=pltpu.CompilerParams(vmem_limit_bytes=16 * 1024 * 1024),
    )(*args)


def flip(values, axis, mask):
    count = lax.axis_size(axis)
    return lax.ppermute(values, axis, [(i, i ^ mask) for i in range(count)])


def gather_chips(part_list):
    bits = (lax.axis_size("chip") - 1).bit_length()
    held = [{0: part} for part in part_list]
    for step in range(bits):
        for number, blocks in enumerate(held):
            mask = 1 << ((number + step) % bits)
            for j in sorted(blocks):
                blocks[j ^ mask] = flip(blocks[j], "chip", mask)
    return held


def scatter_chips(part_list):
    bits = (lax.axis_size("chip") - 1).bit_length()
    for step in reversed(range(bits)):
        for number, blocks in enumerate(part_list):
            mask = 1 << ((number + step) % bits)
            for j in sorted(blocks, reverse=True):
                if j & mask:
                    blocks[j ^ mask] = blocks[j ^ mask] + flip(blocks.pop(j), "chip", mask)
    return [blocks[0] for blocks in part_list]


def body(design, observations, start_coefs, precond, taps):
    chips = lax.axis_size("chip")
    layers = lax.axis_size("coef")
    chip = lax.axis_index("chip")
    core = lax.axis_index("core")
    layer = lax.axis_index("coef")
    arcs = 2 * chips
    arc = 2 * chip + core
    ratio = layers // chips
    half = design.shape[1] // 2
    cut = half // 2
    step = design.shape[0]
    length = taps.shape[0]
    total_obs = step * arcs
    rows = observations.shape[0]
    rows_chip = 2 * start_coefs.shape[0]
    ahead, behind = make_filters(taps)
    inside = jnp.full((8, length), jnp.where(arc + 1 < arcs, 1.0, 0.0), jnp.float32)

    def swap(values, split, join):
        size = values.shape[split] // 2
        keep = lax.dynamic_slice_in_dim(values, core * size, size, split)
        send = lax.dynamic_slice_in_dim(values, (1 - core) * size, size, split)
        other = flip(send, "core", 1)
        low = jnp.where(core == 0, keep, other)
        high = jnp.where(core == 0, other, keep)
        return jnp.concatenate([low, high], axis=join)

    def spot(s):
        z = layer ^ s
        return ((z // ratio) ^ chip) * rows_chip + (z % ratio) * rows

    def stack(held, axis):
        return jnp.concatenate(
            [jnp.concatenate([blocks[j] for blocks in held], axis=axis) for j in range(chips)],
            axis=0,
        )

    def forward(held, axis=1):
        gathered = pieces(stack(held, axis))
        other = flip(product(gathered, far, ((1,), (1,))), "core", 1)
        partial = product(gathered, near, ((1,), (1,))) + other
        ends = jnp.concatenate([partial[:, :length], partial[:, -length:]], axis=1)
        groups = []
        for group in (ends, partial[:, length:-length]):
            parts = [lax.dynamic_slice_in_dim(group, spot(0), rows, 0)]
            for s in range(1, layers):
                parts.append(flip(lax.dynamic_slice_in_dim(group, spot(s), rows, 0), "coef", s))
            groups.append(parts)
        return groups

    def halo(head, tail):
        up = [(a, a + 1) for a in range(arcs - 1)]
        down = [(a + 1, a) for a in range(arcs - 1)]
        left = lax.ppermute(tail, ("chip", "core"), up)
        right = lax.ppermute(head, ("chip", "core"), down)
        return left, right

    def time_sum(table):
        other = flip(table, "core", 1)
        table = table + other
        return [table] + [flip(table, "chip", j) for j in range(1, chips)]

    def full_sum(table):
        parts = time_sum(table)
        total = parts[0]
        for part in parts[1:]:
            total = total + part
        return to_layers(total)

    def to_layers(values):
        return [values] + [flip(values, "coef", s) for s in range(1, layers)]

    def backward(block, *halves):
        other = pieces(flip(block, "core", 1))
        block = halves
        lists = []
        for number in range(2):
            piece = slice(number * cut, (number + 1) * cut)
            partial = product(block, [t[:, piece] for t in near], ((1,), (0,)))
            partial = partial + product(other, [t[:, piece] for t in far], ((1,), (0,)))
            lists.append({j: partial[j * rows_chip : (j + 1) * rows_chip] for j in range(chips)})
        return scatter_chips(lists)

    keep = lax.dynamic_slice_in_dim(start_coefs, core * half, half, 1)
    other = flip(
        lax.dynamic_slice_in_dim(start_coefs, (1 - core) * half, half, 1), "core", 1
    )
    low = jnp.where(core == 0, keep, other)
    high = jnp.where(core == 0, other, keep)
    held_start = gather_chips([low, high])
    send = lax.dynamic_slice_in_dim(design, (1 - core) * half, half, 1)
    far = flip(send, "core", 1)
    far = pieces(far)
    far = lax.optimization_barrier(far)
    near = pieces(lax.dynamic_slice_in_dim(design, core * half, half, 1))
    near = lax.optimization_barrier(near)
    scale_own = lax.dynamic_slice_in_dim(precond, core * half, half, 0)

    def join_ends(*parts):
        both = parts[0]
        for part in parts[1:]:
            both = both + part
        return both[:, :length], both[:, length:]

    def begin_ends(target, *parts):
        head, tail = join_ends(*parts)
        return target[:, :length] - head, target[:, -length:] - tail

    def join(head, tail, *parts):
        middle = parts[0]
        for part in parts[1:]:
            middle = middle + part
        return jnp.concatenate([head, middle, tail], axis=1)

    def first_sums(left, head, tail, right, ahead, target, *parts):
        middle = target[:, length:-length]
        for part in parts:
            middle = middle - part
        residual = jnp.concatenate([head, middle, tail], axis=1)
        whitened = conv(jnp.concatenate([left, residual, right], axis=1), ahead)
        mine = whitened[:, :step]
        return residual, whitened, to_table([dot_rows(mine, mine)], length)

    def robust(whitened, scale, inside, behind):
        weights = 1.0 / jnp.sqrt(
            1.0 + whitened * whitened / (huber_square * scale + epsilon)
        )
        marked = weights * whitened
        marked = jnp.concatenate(
            [marked[:, :step], marked[:, step:] * inside[:1, :]], axis=1
        )
        return weights[:, :step], conv(marked, behind)

    def first_back(shared, blocks):
        inside, behind = shared
        whitened, table = blocks
        scale = table.T[:, 0:1] / total_obs
        weights, back = robust(whitened, scale, inside, behind)
        return back, (weights, back)

    def image_sums(left, head, tail, right, ahead, back, weights, whitened, *rest):
        image = join(head, tail, *rest[:layers])
        previous = rest[layers:]
        imaged = conv(jnp.concatenate([left, image, right], axis=1), ahead)
        mine = imaged[:, :step]
        heavy = weights * mine
        columns = [dot_rows(back, image), dot_rows(heavy, mine)]
        if previous:
            old_image, old_imaged = previous
            old = old_imaged[:, :step]
            columns += [
                dot_rows(back, old_image),
                dot_rows(heavy, old),
                dot_rows(weights * old, old),
            ]
        else:
            columns += [dot_rows(whitened[:, :step], mine), dot_rows(mine, mine)]
        return image, imaged, to_table(columns, length)

    shape = (rows, step)
    wide = (rows, step + length)
    thin = (rows, length)
    small = (8, rows)

    def project(held):
        ends, middle = forward(held)
        head, tail = local(join_ends, (thin, thin), *ends)
        left, right = halo(head, tail)
        return (left, head, tail, right), middle

    ends, middle = forward(held_start, 0)
    head, tail = local(begin_ends, (thin, thin), observations, *ends)
    left, right = halo(head, tail)
    residual, whitened, table = local(
        first_sums, (shape, wide, small), left, head, tail, right, ahead, observations, *middle
    )
    spots = jnp.stack([spot(s) for s in range(layers)]).astype(jnp.int32)
    whitened = to_layers(whitened)
    scale_tables = full_sum(table)
    block, high, low, weights, back = spread_kernel(
        first_back, layers, (shape, shape), spots, (inside, behind), whitened, scale_tables
    )

    def descend(*blocks):
        found = jnp.concatenate(backward(*blocks), axis=1) * scale_own[None, :]
        return found, gather_chips([found[:, :cut], found[:, cut:]])

    first_grad, held = descend(block, high, low)
    sides, middle = project(held)
    image, imaged, table = local(
        image_sums, (shape, wide, small), *sides, ahead, back, weights, whitened[0], *middle
    )
    all_imaged = to_layers(imaged)
    tables = full_sum(table)

    def first_step(shared, blocks):
        inside, behind = shared
        whitened, imaged, table, old = blocks
        sums = table.T
        gp, curve, cross, square = (sums[:, i : i + 1] for i in range(4))
        alpha = gp / curve
        whitened = whitened - alpha * imaged
        scale = old.T[:, 0:1] + alpha * (alpha * square - 2.0 * cross)
        scale = jnp.maximum(scale, 0.0) / total_obs
        weights, back = robust(whitened, scale, inside, behind)
        return back, (weights, back, jnp.broadcast_to(alpha, thin), jnp.broadcast_to(gp, thin))

    block, high, low, weights, back, old_alpha, old_gp = spread_kernel(
        first_step,
        layers,
        (shape, shape, thin, thin),
        spots,
        (inside, behind),
        whitened,
        all_imaged,
        tables,
        scale_tables,
    )

    second_grad, held = descend(block, high, low)
    old_image, old_imaged = image, imaged
    sides, middle = project(held)
    image, imaged, table = local(
        image_sums,
        (shape, wide, small),
        *sides,
        ahead,
        back,
        weights,
        whitened[0],
        *middle,
        old_image,
        old_imaged,
    )
    tables = time_sum(table)

    def second_step(residual, image, old_image, old_alpha, old_gp, *parts):
        sums = from_table(parts)
        gp, new, gd, cross, old = (sums[:, i : i + 1] for i in range(5))
        beta = gp / old_gp[:, :1]
        curve = new + beta * (2.0 * cross + beta * old)
        alpha = (gp + beta * gd) / curve
        residual = residual - old_alpha[:, :1] * old_image - alpha * (image + beta * old_image)
        lengths = jnp.concatenate([old_alpha[:, :1] + alpha * beta, alpha], axis=1)
        return residual, jnp.pad(lengths, ((0, 0), (0, length - 2)))

    misfit, lengths = local(
        second_step, (shape, thin), residual, image, old_image, old_alpha, old_gp, *tables
    )

    per = arcs // layers
    pairs = []
    for a in range(arcs):
        for z in range(layers):
            goal = (z * per + a % per) * layers + a // per
            pairs.append((a * layers + z, goal))
    lengths = lax.ppermute(lengths, ("chip", "core", "coef"), pairs)
    few = start_coefs.shape[0]
    lengths = lax.dynamic_slice_in_dim(lengths, (arc % per) * few, few, 0)
    coefs = start_coefs
    for number, part in enumerate((first_grad, second_grad)):
        coefs = coefs + lengths[:, number : number + 1] * swap(part, 0, 1)
    return coefs, misfit


def solution(mesh):
    arcs, layers = mesh.devices.shape
    inner = Mesh(mesh.devices.reshape(arcs // 2, 2, layers), ("chip", "core", "coef"))
    arc = ("chip", "core")
    placed = (P(arc, "coef"), P("coef", arc), P(arc, "coef"), P("coef"), P())

    return jax.shard_map(
        body,
        mesh=inner,
        in_specs=placed,
        out_specs=(P(arc, "coef"), P("coef", arc)),
        check_vma=False,
    )
```
